1024 devices in a mesh: aisle: 32 (over x, z_hi, core), row: 32 (over y, z_lo).
Axes of the slice: x: 8, y: 8, z: 8 (z_hi: 2, z_lo: 4; z = z_hi * 4 + z_lo), core: 2. Of those that a mesh axis runs over, the one named last changes fastest.
Arguments:
- source: float32 [8, 512, 4096], P(None, 'row', 'aisle'), may hold values from -6 to 6
- conduct: float32 [8, 512, 4096], P(None, 'row', 'aisle'), may hold values from 1 to 10
- solid: int32 [8, 512, 4096], P(None, 'row', 'aisle'), may hold values 0 or 1
Outputs:
- correction: float32 [8, 512, 4096], P(None, 'row', 'aisle')
The draws below stay inside these ranges and needn't reach their ends.
All inputs are finite; a program needn't handle non-finite values. No bound on the sum of `solid` on one device may be relied on, other than what follows from the above.
Results may differ from the reference program's by a relative error of at most 0.0003.
Values sent between devices are 32-bit elements; how exact they have to be, the bound alone decides.
A program may use at most 32 MiB of HBM per device.

```python
import math
import jax
import jax.numpy as jnp
from jax import lax

NZ = 8
CR = 16
CA = 128
OV = 2
SWEEPS = 6
NR = 512
NA = 4096
N_AISLE = 32
N_ROW = 32


def draw_source(key, part):
    rough_key = jax.random.fold_in(key, 11)
    return jax.random.truncated_normal(rough_key, -6.0, 6.0, (NZ, NR, NA), jnp.float32)


def touch_ends(entries, stream_key, low, high):
    index_at = [jax.random.randint(jax.random.fold_in(stream_key, axis), (), 0, length) for axis, length in enumerate(entries.shape)]
    widest = entries.shape.index(max(entries.shape))
    neighbour = index_at[:widest] + [(index_at[widest] + 1) % entries.shape[widest]] + index_at[widest + 1:]
    return entries.at[tuple(index_at)].set(low).at[tuple(neighbour)].set(high)


def levels(rng, shape, shards, least, largest):
    level = 1.0
    for axis_at, parts in shards:
        steps = jax.random.uniform(jax.random.fold_in(jax.random.fold_in(rng, 6), axis_at), (parts,), jnp.float32, least / len(shards), largest / len(shards))
        level = level * jnp.repeat(jnp.exp(steps), shape[axis_at] // parts).reshape((-1,) + (1,) * (len(shape) - 1 - axis_at))
    return level


def setup_inputs(seed: int = 0) -> dict:
    splits = jax.random.split(jax.random.key(seed), 4)
    source = draw_source(jax.random.fold_in(splits[3], 71), 0)
    conduct = jnp.clip(jnp.exp(math.log(10.0) - 2.3025851 * jax.random.uniform(splits[1], (NZ, NR, NA), jnp.float32) ** levels(splits[1], (NZ, NR, NA), ((1, 32), (2, 32)), -0.2, 0.2)), 1.0, 10.0)
    solid = touch_ends((jax.random.randint(splits[2], (NZ, NR, NA), 0, 4) < 1).astype(jnp.int32), jax.random.fold_in(splits[2], 1), 0, 1)
    return {"source": source, "conduct": conduct, "solid": solid}


lower_end = 0.2
upper_end = 2.0


def padded(values):
    return jnp.pad(values, [(0, 0)] * (values.ndim - 3) + [(1, 1)] * 3)


def beside(padded_values):
    return [padded_values[..., 2:, 1:-1, 1:-1], padded_values[..., :-2, 1:-1, 1:-1],
            padded_values[..., 1:-1, 2:, 1:-1], padded_values[..., 1:-1, :-2, 1:-1],
            padded_values[..., 1:-1, 1:-1, 2:], padded_values[..., 1:-1, 1:-1, :-2]]


def coupling(padded_cond, shift_term):
    centre = padded_cond[..., 1:-1, 1:-1, 1:-1]
    weights = [0.5 * (centre + other) for other in beside(padded_cond)]
    diagonal = shift_term
    for weight in weights:
        diagonal = diagonal + weight
    return weights, diagonal


def operate(padded_values, weights, diagonal):
    others = beside(padded_values)
    summed = weights[0] * others[0]
    for number in range(1, 6):
        summed = summed + weights[number] * others[number]
    return diagonal * padded_values[..., 1:-1, 1:-1, 1:-1] - summed


def smooth_local(source_ext, weights, diagonal):
    middle = 0.5 * (upper_end + lower_end)
    spread = 0.5 * (upper_end - lower_end)
    ratio_now = spread / middle
    inverse = 1.0 / diagonal
    update = inverse * source_ext / middle
    estimate = update
    for sweep_no in range(SWEEPS):
        remain = source_ext - operate(padded(estimate), weights, diagonal)
        ratio_next = 1.0 / (2.0 * middle / spread - ratio_now)
        update = (ratio_next * ratio_now) * update + (2.0 * ratio_next / spread) * inverse * remain
        estimate = estimate + update
        ratio_now = ratio_next
    return estimate


def schwarz(source, cond, shift_term):
    total_cols = CA * N_AISLE
    width_rows = CR + 2 * OV
    cond_rows = jnp.pad(cond, ((0, 0), (OV, OV), (0, 0)))
    shift_rows = jnp.pad(shift_term, ((0, 0), (OV, OV), (0, 0)), constant_values=1.0)
    source_rows = jnp.pad(source, ((0, 0), (OV, OV), (0, 0)))
    table = ((jnp.arange(N_AISLE, dtype=jnp.int32)[:, None] * CA - OV
              + jnp.arange(CA + 2 * OV, dtype=jnp.int32)[None, :]) % total_cols).astype(jnp.int32)
    core_mask = jnp.pad(jnp.ones((CR, CA), jnp.float32), OV)

    def blocks(slab):
        return jnp.moveaxis(jnp.take(slab, table, axis=2), 2, 0)

    def step(total, block_row):
        start = (block_row * CR).astype(jnp.int32)

        def cut(values):
            return lax.dynamic_slice_in_dim(values, start, width_rows, axis=1)

        weights, diagonal = coupling(padded(blocks(cut(cond_rows))), blocks(cut(shift_rows)))
        result = smooth_local(blocks(cut(source_rows)) * core_mask, weights, diagonal)
        folded = jnp.zeros((NZ, width_rows, total_cols), jnp.float32).at[:, :, table].add(jnp.moveaxis(result, 0, 2))
        current = lax.dynamic_slice_in_dim(total, start, width_rows, axis=1)
        total = lax.dynamic_update_slice_in_dim(total, current + folded, start, axis=1)
        return total, None

    total = jnp.zeros((NZ, CR * N_ROW + 2 * OV, total_cols), jnp.float32)
    total, unused = lax.scan(step, total, jnp.arange(N_ROW, dtype=jnp.int32))
    return total[:, OV:OV + CR * N_ROW, :]


def wrap_pad(values):
    with_cols = jnp.concatenate([values[..., -1:], values, values[..., :1]], axis=-1)
    return jnp.pad(with_cols, ((1, 1), (1, 1), (0, 0)))


def reference(source, conduct, solid):
    shift_term = 0.05 + 20.0 * solid.astype(jnp.float32)
    first = schwarz(source, conduct, shift_term)
    weights, diagonal = coupling(wrap_pad(conduct), shift_term)
    remain = source - operate(wrap_pad(first), weights, diagonal)
    return first + schwarz(remain, conduct, shift_term)
```

```python
import functools
import math

import jax
import jax.numpy as jnp
from jax import lax
from jax.experimental import pallas as pl
from jax.experimental.pallas import tpu as pltpu
from jax.sharding import PartitionSpec as P

MESH = pl.DeviceIdType.MESH
NZ, ROWS, COLS = 8, 16, 128

MIDDLE, SPREAD, STEPS = 1.1, 0.9, 7
ORDER = (4, 1, 7, 3, 5, 2, 6)
TAUS = tuple(1.0 / (MIDDLE + SPREAD * math.cos(math.pi * (2 * k - 1) / (2 * STEPS))) for k in ORDER)

FIRST_ROW = (-13, -2, 14)
LENGTH = (15, 20, 15)
SKEW = (40, 0, 88)
BASE = (0, 15, 35)
SIDE = 50
TILES = 70
K_ROWS = (range(-14, 2), range(-2, 18), range(14, 30))


def roll(x, by):
    by = by % COLS
    return x if by == 0 else pltpu.roll(x, by, 1)


def vroll(x, by):
    return pltpu.roll(x, by % NZ, 0)


def kernel(src_hbm, cond_hbm, solid_hbm, out_ref,
           own_src, own_cond, own_solid, to_side, ns_src, ns_cond, ns_solid, from_side,
           half, half_side, wgt, rhs, est, first,
           load_sem, send_sem, recv_sem):
    n_a, n_r = lax.axis_size("aisle"), lax.axis_size("row")
    a, r = lax.axis_index("aisle"), lax.axis_index("row")
    has_n, has_s = r > 0, r < n_r - 1

    def device(da, dr):
        return {"aisle": lax.rem(a + (da + n_a), n_a), "row": lax.rem(r + (dr + n_r), n_r)}

    loads = [
        pltpu.make_async_copy(h, v, load_sem.at[i])
        for i, (h, v) in enumerate(((cond_hbm, own_cond), (solid_hbm, own_solid), (src_hbm, own_src)))
    ]
    for c in loads:
        c.start()

    around = [(da, dr) for da in (-1, 0, 1) for dr in (-1, 0, 1) if (da, dr) != (0, 0)]
    barrier = pltpu.get_barrier_semaphore()
    for da, dr in around:
        pl.semaphore_signal(barrier, inc=1, device_id=device(da, dr), device_id_type=MESH)

    lane = lax.broadcasted_iota(jnp.int32, (NZ, COLS), 1)
    level = lax.broadcasted_iota(jnp.int32, (NZ, COLS), 0)
    rel = [lax.rem(lane + (COLS - s), COLS) for s in SKEW]
    mine = [(q < 18) | (q >= 110) for q in rel]
    relx = jnp.where(mine[0], rel[0], jnp.where(mine[2], rel[2], rel[1]))
    band = jnp.where(mine[0], 0, jnp.where(mine[2], 2, 1))
    code = band * COLS + relx
    zero = jnp.zeros((NZ, COLS), jnp.float32)
    one = jnp.ones((NZ, COLS), jnp.float32)

    def own_row(kind, row):
        rows = pl.ds(row, NZ, stride=ROWS)
        if kind == 0:
            return own_cond[rows, :]
        if kind == 1:
            return 0.05 + 20.0 * own_solid[rows, :].astype(jnp.float32)
        return own_src[rows, :]

    for c in loads:
        c.wait()
    slot = lax.div(lane, 16)
    for kind in range(3):
        for half_of in range(2):
            west, east = zero, zero
            for s in range(8):
                v = own_row(kind, half_of * 8 + s)
                here = slot == s
                west = jnp.where(here, roll(v, 16 * s), west)
                east = jnp.where(here, roll(v, 16 * s + 14), east)
            to_side[0, kind * 2 + half_of] = west
            to_side[1, kind * 2 + half_of] = east

    pl.semaphore_wait(barrier, len(around))

    copies = []

    def send(source, target, n, da, dr):
        c = pltpu.make_async_remote_copy(
            src_ref=source, dst_ref=target, send_sem=send_sem.at[n], recv_sem=recv_sem.at[n],
            device_id=device(da, dr), device_id_type=MESH)
        c.start()
        copies.append(c)

    n = 0
    for dr in (-1, 1, 0):
        for da in (-1, 1):
            send(to_side.at[0 if da < 0 else 1], from_side.at[(3 if da < 0 else 0) + 1 - dr], n, da, dr)
            n += 1
    for dr in (-1, 1):
        where = 1 if dr < 0 else 0
        for source, target in ((cond_hbm, ns_cond), (solid_hbm, ns_solid), (src_hbm, ns_src)):
            send(source, target.at[where], n, 0, dr)
            n += 1
    for c in copies:
        c.wait_recv()

    fill = (zero, one, zero)

    def main_row(kind, row):
        if 0 <= row < ROWS:
            return own_row(kind, row)
        w, exists = (0, has_n) if row < 0 else (1, has_s)
        rows = pl.ds(row % ROWS, NZ, stride=ROWS)
        if kind == 0:
            v = ns_cond[w, rows, :]
        elif kind == 1:
            v = 0.05 + 20.0 * ns_solid[w, rows, :].astype(jnp.float32)
        else:
            v = ns_src[w, rows, :]
        return jnp.where(exists, v, fill[kind])

    def strips(kind, row):
        which = 0 if row < 0 else (1 if row < ROWS else 2)
        q = row % ROWS
        return from_side[which, kind * 2 + q // 8], from_side[3 + which, kind * 2 + q // 8], 16 * (q % 8)

    def side_tile(kind, j, mains):
        tile = fill[kind]
        for g in range(3):
            row = FIRST_ROW[g] + j
            if row not in K_ROWS[g] or (kind and not 0 <= j < LENGTH[g]):
                continue
            in_core = (row < 0, 0 <= row < ROWS, row >= ROWS)[g]
            if kind == 2 and not in_core:
                continue
            at = g * COLS
            w, e, off = strips(kind, row)
            part = jnp.where(relx < 64, roll(e, 4 + SKEW[g] - off), roll(w, SKEW[g] - 18 - off))
            if kind == 2:
                keep = ((code >= at + 4) & (code < at + 18)) | ((code >= at + 110) & (code < at + 124))
                part = jnp.where(keep, part, 0.0)
            else:
                m = mains[g]
                own = jnp.where(relx < 64, roll(m, 4), roll(m, -4))
                part = jnp.where((relx < 4) | (relx >= 124), own, part)
            exists = has_n if row < 0 else (has_s if row >= ROWS else None)
            if exists is not None:
                part = jnp.where(exists, part, fill[kind])
            tile = jnp.where((band == g) & mine_any, part, tile)
        if kind != 2:
            tile = jnp.where(relx < 2, roll(tile, -4), jnp.where(relx >= 126, roll(tile, 4), tile))
            tile = jnp.where(mine_any, tile, fill[kind])
        return tile

    mine_any = mine[0] | mine[1] | mine[2]

    def hidx(g, j):
        return (0, 16, 36)[g] + j + (1 if g == 0 else 0)

    for j in range(-1, 20):
        mains = {}
        for g in range(3):
            row = FIRST_ROW[g] + j
            if row in K_ROWS[g]:
                mains[g] = roll(main_row(0, row), SKEW[g])
                half[hidx(g, j)] = 0.5 * mains[g]
        half_side[j + 1] = 0.5 * side_tile(0, j, mains)

    def around_cols(mains, side):
        sp, sm = roll(side, -1), roll(side, 1)
        out, plus, minus = {}, sp, sm
        for g, m in mains.items():
            mp, mm = roll(m, -1), roll(m, 1)
            out[g] = (jnp.where(rel[g] == 127, sp, mp), jnp.where(rel[g] == 0, sm, mm))
            plus = jnp.where(code == g * COLS + 127, mp, plus)
            minus = jnp.where(code == g * COLS, mm, minus)
        out[3] = (plus, minus)
        return out

    top, bottom = level == NZ - 1, level == 0
    no_plus = (relx == 1) | (relx == 125)
    no_minus = (relx == 2) | (relx == 126)
    live = mine_any & ((relx < 17) | (relx > 110))

    def weights(at, h, s, up, down, plus, minus, side, alive):
        vp = h + jnp.where(top, 0.0, vroll(h, -1))
        vm = h + jnp.where(bottom, 0.0, vroll(h, 1))
        rp = h + down
        rm = h + up
        cp = h + (jnp.where(no_plus, 0.0, plus) if side else plus)
        cm = h + (jnp.where(no_minus, 0.0, minus) if side else minus)
        inverse = 1.0 / ((((((s + vp) + vm) + rp) + rm) + cp) + cm)
        if side:
            inverse = jnp.where(alive, inverse, 0.0)
        wgt[0, at] = jnp.where(top, 0.0, inverse * vp)
        wgt[1, at] = jnp.where(bottom, 0.0, inverse * vm)
        wgt[2, at] = inverse * rp
        wgt[3, at] = inverse * rm
        cp, cm = inverse * cp, inverse * cm
        wgt[4, at] = jnp.where(no_plus, 0.0, cp) if side else cp
        wgt[5, at] = jnp.where(no_minus, 0.0, cm) if side else cm
        return inverse

    tau0 = TAUS[0]
    for j in range(20):
        bands = [g for g in range(3) if j < LENGTH[g]]
        mains = {g: half[hidx(g, j)] for g in bands}
        side = half_side[j + 1]
        cols = around_cols(mains, side)
        shifts = {}
        for g in bands:
            row = FIRST_ROW[g] + j
            shifts[g] = roll(main_row(1, row), SKEW[g])
            up = half[hidx(g, j - 1)] if row - 1 in K_ROWS[g] else zero
            down = half[hidx(g, j + 1)] if row + 1 in K_ROWS[g] else zero
            inverse = weights(BASE[g] + j, mains[g], shifts[g], up, down, *cols[g], False, None)
            if (row < 0, 0 <= row < ROWS, row >= ROWS)[g]:
                b = inverse * roll(main_row(2, row), SKEW[g])
            else:
                b = zero
            rhs[BASE[g] + j] = b
            est[BASE[g] + j] = tau0 * b
        alive = live
        if len(bands) == 1:
            alive = live & (band == 1)
        up = half_side[j]
        if j == 0:
            up = jnp.where(band == 0, up, 0.0)
        down = half_side[j + 2] if j < 19 else zero
        inverse = weights(SIDE + j, side, side_tile(1, j, shifts), up, down, *cols[3], True, alive)
        b = inverse * side_tile(2, j, None)
        rhs[SIDE + j] = b
        est[SIDE + j] = tau0 * b

    def stencil(ref, b, spans, emit):
        def load(g, j):
            if g == 3:
                return ref[SIDE + j] if 0 <= j < 20 else None
            return ref[BASE[g] + j] if j in spans[g] else None

        old = {(g, j): load(g, j) for g in range(4) for j in (-1, 0)}
        for j in range(20):
            for g in range(4):
                old[g, j + 1] = load(g, j + 1)
            mains = {g: old[g, j] for g in range(3) if old[g, j] is not None}
            cols = around_cols(mains, old[3, j])
            for g in (*mains, 3):
                at = (SIDE if g == 3 else BASE[g]) + j
                x = old[g, j]
                plus, minus = cols[g]
                total = b[at] + wgt[0, at] * vroll(x, -1)
                other = wgt[1, at] * vroll(x, 1)
                if old[g, j + 1] is not None:
                    total = total + wgt[2, at] * old[g, j + 1]
                if old[g, j - 1] is not None:
                    other = other + wgt[3, at] * old[g, j - 1]
                total = total + wgt[4, at] * plus
                other = other + wgt[5, at] * minus
                emit(at, g, j, total + other, x)

    def solve(spans):
        def sweep(t, carry):
            tau = jnp.float32(TAUS[STEPS - 1])
            for i in range(STEPS - 2, 0, -1):
                tau = jnp.where(t == i, jnp.float32(TAUS[i]), tau)

            def emit(at, g, j, total, x):
                est[at] = x + tau * (total - x)

            stencil(est, rhs, spans, emit)
            return carry

        lax.fori_loop(1, STEPS, sweep, 0)

    full = [range(n) for n in LENGTH]
    solve(full)

    def gather_rows(g, j):
        v = est[BASE[g] + j]
        if g == 1 and j < 4:
            v = v + roll(est[BASE[0] + j + 11], -SKEW[0])
        if g == 1 and j >= 16:
            v = v + roll(est[BASE[2] + j - 16], -SKEW[2])
        if g == 0 and j >= 11:
            v = v + roll(est[BASE[1] + j - 11], SKEW[0])
        if g == 2 and j < 4:
            v = v + roll(est[BASE[1] + j + 16], SKEW[2])
        return v

    def gather_rows_side(j):
        v = est[SIDE + j]
        if j < 4:
            v = v + jnp.where(band == 1, roll(est[SIDE + j + 11], -SKEW[0]), 0.0)
            v = v + jnp.where(band == 2, roll(est[SIDE + j + 16], SKEW[2]), 0.0)
        if j >= 16:
            v = v + jnp.where(band == 1, roll(est[SIDE + j - 16], -SKEW[2]), 0.0)
        if 11 <= j < 15:
            v = v + jnp.where(band == 0, roll(est[SIDE + j - 11], SKEW[0]), 0.0)
        return jnp.where(mine_any, v, 0.0)

    near = [range(6, 15), range(0, 20), range(0, 9)]
    from_minus = (relx == 126) | (relx == 127) | (relx == 4) | (relx == 5)
    from_plus = (relx == 122) | (relx == 123) | (relx == 0) | (relx == 1)
    from_main_minus = (relx == 2) | (relx == 3)
    from_main_plus = (relx == 124) | (relx == 125)
    for j in range(20):
        side = gather_rows_side(j)
        s4, s_4 = roll(side, 4), roll(side, -4)
        add = jnp.where(from_minus, s4, jnp.where(from_plus, s_4, 0.0))
        exists = has_n if j < 2 else (has_s if j >= 18 else None)
        for g in range(3):
            if j not in near[g]:
                continue
            m = gather_rows(g, j)
            f = m + jnp.where(rel[g] < 2, s4, jnp.where(rel[g] >= 126, s_4, 0.0))
            cross = jnp.where(from_main_minus, roll(m, 4), jnp.where(from_main_plus, roll(m, -4), add))
            add = jnp.where(band == g, cross, add)
            if g == 1 and exists is not None:
                f = jnp.where(exists, f, 0.0)
            first[BASE[g] + j] = f
        f = side + add
        if exists is not None:
            f = jnp.where((band != 1) | exists, f, 0.0)
        first[SIDE + j] = f

    core_lane = ((relx >= 4) & (relx < 17)) | ((relx > 110) & (relx < 124))

    def emit_rhs(at, g, j, total, x):
        b = total - x
        if g == 3:
            keep = core_lane & mine_any
            use = []
            if 7 <= j <= 12:
                use.append((band == 0) & has_n)
            if 2 <= j <= 17:
                use.append(band == 1)
            if 2 <= j <= 7:
                use.append((band == 2) & has_s)
            if not use:
                b = zero
            else:
                any_use = use[0]
                for u in use[1:]:
                    any_use = any_use | u
                b = jnp.where(keep & any_use, b, 0.0)
        elif g == 0:
            b = jnp.where(has_n, b, 0.0) if 7 <= j <= 12 else zero
        elif g == 2:
            b = jnp.where(has_s, b, 0.0) if 2 <= j <= 7 else zero
        elif not 2 <= j <= 17:
            b = zero
        rhs[at] = b
        est[at] = tau0 * b

    stencil(first, rhs, near, emit_rhs)

    solve([range(7, 15), range(0, 20), range(0, 8)])

    for j in range(2, 18):
        side = est[SIDE + j]
        if j < 4:
            side = side + roll(est[SIDE + j + 11], -SKEW[0])
        if j >= 16:
            side = side + roll(est[SIDE + j - 16], -SKEW[2])
        v = first[BASE[1] + j] + gather_rows(1, j)
        v = v + jnp.where(lane < 2, roll(side, 4), jnp.where(lane >= 126, roll(side, -4), 0.0))
        out_ref[pl.ds(j - 2, NZ, stride=ROWS), :] = v

    for c in copies:
        c.wait_send()


def body(source, conduct, solid):
    flat = (NZ * ROWS, COLS)
    f32, i32 = jnp.float32, jnp.int32
    tile = (NZ, COLS)
    out = pl.pallas_call(
        kernel,
        out_shape=jax.ShapeDtypeStruct(flat, f32),
        in_specs=[pl.BlockSpec(memory_space=pltpu.HBM)] * 3,
        out_specs=pl.BlockSpec(memory_space=pltpu.VMEM),
        scratch_shapes=[
            pltpu.VMEM(flat, f32), pltpu.VMEM(flat, f32), pltpu.VMEM(flat, i32),
            pltpu.VMEM((2, 6, *tile), f32),
            pltpu.VMEM((2, *flat), f32), pltpu.VMEM((2, *flat), f32), pltpu.VMEM((2, *flat), i32),
            pltpu.VMEM((6, 6, *tile), f32),
            pltpu.VMEM((52, *tile), f32), pltpu.VMEM((21, *tile), f32),
            pltpu.VMEM((6, TILES, *tile), f32),
            pltpu.VMEM((TILES, *tile), f32), pltpu.VMEM((TILES, *tile), f32), pltpu.VMEM((TILES, *tile), f32),
            pltpu.SemaphoreType.DMA((3,)), pltpu.SemaphoreType.DMA((12,)), pltpu.SemaphoreType.DMA((12,)),
        ],
        compiler_params=pltpu.CompilerParams(
            collective_id=0, has_side_effects=True, vmem_limit_bytes=16 * 1024 * 1024),
    )(*(pltpu.with_memory_space_constraint(x.reshape(flat), pltpu.HBM) for x in (source, conduct, solid)))
    return out.reshape(source.shape)


def solution(mesh):
    spec = P(None, "row", "aisle")
    return jax.shard_map(body, mesh=mesh, in_specs=(spec, spec, spec), out_specs=spec, check_vma=False)
```

```python
import functools
import math

import jax
import jax.numpy as jnp
from jax import lax
from jax.experimental import pallas as pl
from jax.experimental.pallas import tpu as pltpu
from jax.sharding import PartitionSpec as P

MESH = pl.DeviceIdType.MESH
NZ, ROWS, COLS = 8, 16, 128

MIDDLE, SPREAD, STEPS = 1.1, 0.9, 7
CHUNK = (4, 2, 4, 8, 2, 7)
ORDER = (4, 1, 7, 3, 5, 2, 6)
TAUS = tuple(1.0 / (MIDDLE + SPREAD * math.cos(math.pi * (2 * k - 1) / (2 * STEPS))) for k in ORDER)

FIRST_ROW = (-13, -2, 14)
LENGTH = (15, 20, 15)
SKEW = (40, 0, 88)
BASE = (0, 15, 35)
SIDE = 50
TILES = 70
K_ROWS = (range(-14, 2), range(-2, 18), range(14, 30))


def roll(x, by):
    by = by % COLS
    return x if by == 0 else pltpu.roll(x, by, 1)


def vroll(x, by):
    return pltpu.roll(x, by % NZ, 0)


def kernel(src_hbm, cond_hbm, solid_hbm, out_ref,
           own_src, own_cond, own_solid, to_side, ns_src, ns_cond, ns_solid, from_side,
           half, half_side, wgt, rhs, est, first,
           load_sem, send_sem, recv_sem, ready_sem):
    n_a, n_r = lax.axis_size("aisle"), lax.axis_size("row")
    a, r = lax.axis_index("aisle"), lax.axis_index("row")
    has_n, has_s = r > 0, r < n_r - 1

    def device(da, dr):
        return {"aisle": lax.rem(a + (da + n_a), n_a), "row": lax.rem(r + (dr + n_r), n_r)}

    loads = [
        pltpu.make_async_copy(h, v, load_sem.at[i])
        for i, (h, v) in enumerate(((cond_hbm, own_cond), (solid_hbm, own_solid), (src_hbm, own_src)))
    ]
    for c in loads:
        c.start()

    def order(pos_a, pos_r):
        plane = lax.rem(lax.div(pos_a, 2), 2) * 4 + lax.rem(pos_r, 4)
        return jnp.where((pos_a == 0) & (pos_r == 0), 15, plane * 4 + lax.rem(pos_a, 2) * 2)

    near_side = 1 - 2 * lax.rem(a, 2)
    sides = {"own": 0, "near": near_side, "far": -near_side}
    ways = [("own", 1), ("near", 0), ("near", 1), ("near", -1), ("own", -1), ("far", 0), ("far", 1), ("far", -1)]
    place = {w: i for i, w in enumerate(ways)}

    def order(pos_a, pos_r):
        plane = lax.rem(lax.div(pos_a, 2), 2) * 4 + lax.rem(pos_r, 4)
        return jnp.where((pos_a == 0) & (pos_r == 0), 15, plane * 4 + lax.rem(pos_a, 2) * 2)

    here_at = order(a, r)
    earlier, n_earlier = {}, 0
    for side, dr in ways:
        there = device(sides[side], dr)
        earlier[side, dr] = order(there["aisle"], there["row"]) < here_at
        n_earlier = n_earlier + earlier[side, dr].astype(jnp.int32)
    barrier = pltpu.get_barrier_semaphore()
    for w in ways:
        @pl.when(jnp.logical_not(earlier[w]))
        def _():
            pl.semaphore_signal(barrier, inc=1, device_id=device(sides[w[0]], w[1]), device_id_type=MESH)

    @pl.when(n_earlier > 0)
    def _():
        pl.semaphore_wait(barrier, n_earlier)

    for w in ways:
        @pl.when(earlier[w])
        def _():
            pl.semaphore_signal(ready_sem.at[place[w[0], -w[1]]], inc=1, device_id=device(sides[w[0]], w[1]), device_id_type=MESH)

    def blocks(indices, size, do):
        indices = list(indices)
        for at in range(0, len(indices), size):
            @pl.when(r >= 0)
            def _():
                for i in indices[at:at + size]:
                    do(i)

    lane = lax.broadcasted_iota(jnp.int32, (NZ, COLS), 1)
    level = lax.broadcasted_iota(jnp.int32, (NZ, COLS), 0)
    rel = [lax.rem(lane + (COLS - s), COLS) for s in SKEW]
    mine = [(q < 18) | (q >= 110) for q in rel]
    relx = jnp.where(mine[0], rel[0], jnp.where(mine[2], rel[2], rel[1]))
    band = jnp.where(mine[0], 0, jnp.where(mine[2], 2, 1))
    code = band * COLS + relx
    zero = jnp.zeros((NZ, COLS), jnp.float32)
    one = jnp.ones((NZ, COLS), jnp.float32)

    def own_row(kind, row):
        rows = pl.ds(row, NZ, stride=ROWS)
        if kind == 0:
            return own_cond[rows, :]
        if kind == 1:
            return 0.05 + 20.0 * own_solid[rows, :].astype(jnp.float32)
        return own_src[rows, :]

    for c in loads:
        c.wait()
    slot = lax.div(lane, 16)
    def pack(i):
        kind, half_of = divmod(i, 2)
        west, east = zero, zero
        for s in range(8):
            v = own_row(kind, half_of * 8 + s)
            here = slot == s
            west = jnp.where(here, roll(v, 16 * s), west)
            east = jnp.where(here, roll(v, 16 * s + 14), east)
        to_side[0, i] = west
        to_side[1, i] = east

    blocks(range(6), CHUNK[4], pack)

    copies, n = {}, 0
    for side, dr in ways:
        if side == "own":
            w = 1 if dr < 0 else 0
            pairs = [(cond_hbm, ns_cond.at[w]), (solid_hbm, ns_solid.at[w]), (src_hbm, ns_src.at[w])]
        else:
            east = lax.div(sides[side] + 1, 2)
            pairs = [(to_side.at[east], from_side.at[3 * (1 - east) + 1 - dr])]
        copies[side, dr] = []
        for source, target in pairs:
            copies[side, dr].append(pltpu.make_async_remote_copy(
                src_ref=source, dst_ref=target, send_sem=send_sem.at[n], recv_sem=recv_sem.at[n],
                device_id=device(sides[side], dr), device_id_type=MESH))
            n += 1
    for w in ways[::-1]:
        @pl.when(earlier[w])
        def _():
            for c in copies[w]:
                c.start()
    def send_later(which):
        for w in which:
            @pl.when(jnp.logical_not(earlier[w]))
            def _():
                pl.semaphore_wait(ready_sem.at[place[w]], 1)
                for c in copies[w]:
                    c.start()

    send_later(ways)
    for dr in (1, -1):
        for c in copies["own", dr]:
            c.wait_recv()

    fill = (zero, one, zero)

    def main_row(kind, row):
        if 0 <= row < ROWS:
            return own_row(kind, row)
        w, exists = (0, has_n) if row < 0 else (1, has_s)
        rows = pl.ds(row % ROWS, NZ, stride=ROWS)
        if kind == 0:
            v = ns_cond[w, rows, :]
        elif kind == 1:
            v = 0.05 + 20.0 * ns_solid[w, rows, :].astype(jnp.float32)
        else:
            v = ns_src[w, rows, :]
        return jnp.where(exists, v, fill[kind])

    def strips(kind, row):
        which = 0 if row < 0 else (1 if row < ROWS else 2)
        q = row % ROWS
        return from_side[which, kind * 2 + q // 8], from_side[3 + which, kind * 2 + q // 8], 16 * (q % 8)

    def side_start(kind, j, mains):
        tile = fill[kind]
        for g, m in mains.items():
            own = jnp.where(relx < 64, roll(m, 4), roll(m, -4))
            tile = jnp.where((band == g) & edge, own, tile)
        return tile

    def side_tile(kind, j, tile):
        for g in range(3):
            row = FIRST_ROW[g] + j
            if row not in K_ROWS[g] or (kind and not 0 <= j < LENGTH[g]):
                continue
            if kind == 2 and not (row < 0, 0 <= row < ROWS, row >= ROWS)[g]:
                continue
            w, e, off = strips(kind, row)
            part = jnp.where(relx < 64, roll(e, 4 + SKEW[g] - off), roll(w, SKEW[g] - 18 - off))
            exists = has_n if row < 0 else (has_s if row >= ROWS else None)
            if exists is not None:
                part = jnp.where(exists, part, fill[kind])
            tile = jnp.where((band == g) & strip, part, tile)
        if kind != 2:
            tile = jnp.where(relx < 2, roll(tile, -4), jnp.where(relx >= 126, roll(tile, 4), tile))
        return jnp.where(mine_any, tile, fill[kind])

    mine_any = mine[0] | mine[1] | mine[2]
    edge = mine_any & ((relx == 2) | (relx == 3) | (relx == 124) | (relx == 125))
    strip = mine_any & (((relx >= 4) & (relx < 18)) | ((relx >= 110) & (relx < 124)))

    def hidx(g, j):
        return (0, 16, 36)[g] + j + (1 if g == 0 else 0)

    def conduct_tiles(j):
        mains = {}
        for g in range(3):
            row = FIRST_ROW[g] + j
            if row in K_ROWS[g]:
                mains[g] = roll(main_row(0, row), SKEW[g])
                half[hidx(g, j)] = 0.5 * mains[g]
        half_side[j + 1] = side_start(0, j, mains)

    blocks(range(-1, 20), CHUNK[0], conduct_tiles)

    top, bottom = level == NZ - 1, level == 0

    def vertical(h):
        return h + jnp.where(top, 0.0, vroll(h, -1)), h + jnp.where(bottom, 0.0, vroll(h, 1))

    def main_tiles(j):
        shifts = {}
        for g in range(3):
            if j >= LENGTH[g]:
                continue
            row, at = FIRST_ROW[g] + j, BASE[g] + j
            shifts[g] = s = roll(main_row(1, row), SKEW[g])
            h = half[hidx(g, j)]
            vp, vm = vertical(h)
            rp = h + (half[hidx(g, j + 1)] if row + 1 in K_ROWS[g] else zero)
            rm = h + (half[hidx(g, j - 1)] if row - 1 in K_ROWS[g] else zero)
            est[at] = (((s + vp) + vm) + rp) + rm
            wgt[0, at] = jnp.where(top, 0.0, vp)
            wgt[1, at] = jnp.where(bottom, 0.0, vm)
            wgt[2, at] = rp
            wgt[3, at] = rm
            if (row < 0, 0 <= row < ROWS, row >= ROWS)[g]:
                rhs[at] = roll(main_row(2, row), SKEW[g])
            else:
                rhs[at] = zero
        est[SIDE + j] = side_start(1, j, shifts)

    blocks(range(20), CHUNK[1], main_tiles)

    for w in ways:
        if w[0] != "own":
            for c in copies[w]:
                c.wait_recv()
    copies = [c for w in ways for c in copies[w]]

    def conduct_side_tiles(j):
        half_side[j + 1] = 0.5 * side_tile(0, j, half_side[j + 1])

    blocks(range(-1, 20), CHUNK[5], conduct_side_tiles)

    def around_cols(mains, side):
        sp, sm = roll(side, -1), roll(side, 1)
        out, plus, minus = {}, sp, sm
        for g, m in mains.items():
            mp, mm = roll(m, -1), roll(m, 1)
            out[g] = (jnp.where(rel[g] == 127, sp, mp), jnp.where(rel[g] == 0, sm, mm))
            plus = jnp.where(code == g * COLS + 127, mp, plus)
            minus = jnp.where(code == g * COLS, mm, minus)
        out[3] = (plus, minus)
        return out

    no_plus = (relx == 1) | (relx == 125)
    no_minus = (relx == 2) | (relx == 126)
    live = mine_any & ((relx < 17) | (relx > 110))

    tau0 = TAUS[0]

    def weight_tiles(j):
        bands = [g for g in range(3) if j < LENGTH[g]]
        mains = {g: half[hidx(g, j)] for g in bands}
        h = half_side[j + 1]
        cols = around_cols(mains, h)
        for g in bands:
            at = BASE[g] + j
            cp, cm = mains[g] + cols[g][0], mains[g] + cols[g][1]
            inverse = 1.0 / ((est[at] + cp) + cm)
            for i in range(4):
                wgt[i, at] = inverse * wgt[i, at]
            wgt[4, at] = inverse * cp
            wgt[5, at] = inverse * cm
            b = inverse * rhs[at]
            rhs[at] = b
            est[at] = tau0 * b
        at = SIDE + j
        up = half_side[j]
        if j == 0:
            up = jnp.where(band == 0, up, 0.0)
        vp, vm = vertical(h)
        rp = h + (half_side[j + 2] if j < 19 else zero)
        rm = h + up
        cp = h + jnp.where(no_plus, 0.0, cols[3][0])
        cm = h + jnp.where(no_minus, 0.0, cols[3][1])
        inverse = 1.0 / ((((((side_tile(1, j, est[at]) + vp) + vm) + rp) + rm) + cp) + cm)
        alive = live if len(bands) == 3 else live & (band == 1)
        inverse = jnp.where(alive, inverse, 0.0)
        wgt[0, at] = jnp.where(top, 0.0, inverse * vp)
        wgt[1, at] = jnp.where(bottom, 0.0, inverse * vm)
        wgt[2, at] = inverse * rp
        wgt[3, at] = inverse * rm
        wgt[4, at] = jnp.where(no_plus, 0.0, inverse * cp)
        wgt[5, at] = jnp.where(no_minus, 0.0, inverse * cm)
        b = inverse * side_tile(2, j, zero)
        rhs[at] = b
        est[at] = tau0 * b

    blocks(range(20), CHUNK[1], weight_tiles)

    def stencil(ref, b, spans, emit):
        def load(g, j):
            if g == 3:
                return ref[SIDE + j] if 0 <= j < 20 else None
            return ref[BASE[g] + j] if j in spans[g] else None

        old = {(g, j): load(g, j) for g in range(4) for j in (-1, 0)}
        for j in range(20):
            for g in range(4):
                old[g, j + 1] = load(g, j + 1)
            mains = {g: old[g, j] for g in range(3) if old[g, j] is not None}
            cols = around_cols(mains, old[3, j])
            for g in (*mains, 3):
                at = (SIDE if g == 3 else BASE[g]) + j
                x = old[g, j]
                plus, minus = cols[g]
                total = b[at] + wgt[0, at] * vroll(x, -1)
                other = wgt[1, at] * vroll(x, 1)
                if old[g, j + 1] is not None:
                    total = total + wgt[2, at] * old[g, j + 1]
                if old[g, j - 1] is not None:
                    other = other + wgt[3, at] * old[g, j - 1]
                total = total + wgt[4, at] * plus
                other = other + wgt[5, at] * minus
                emit(at, g, j, total + other, x)

    def solve(spans):
        def sweep(t, carry):
            tau = jnp.float32(TAUS[STEPS - 1])
            for i in range(STEPS - 2, 0, -1):
                tau = jnp.where(t == i, jnp.float32(TAUS[i]), tau)

            def emit(at, g, j, total, x):
                est[at] = x + tau * (total - x)

            stencil(est, rhs, spans, emit)
            return carry

        lax.fori_loop(1, STEPS, sweep, 0)

    full = [range(n) for n in LENGTH]
    solve(full)

    def gather_rows(g, j):
        v = est[BASE[g] + j]
        if g == 1 and j < 4:
            v = v + roll(est[BASE[0] + j + 11], -SKEW[0])
        if g == 1 and j >= 16:
            v = v + roll(est[BASE[2] + j - 16], -SKEW[2])
        if g == 0 and j >= 11:
            v = v + roll(est[BASE[1] + j - 11], SKEW[0])
        if g == 2 and j < 4:
            v = v + roll(est[BASE[1] + j + 16], SKEW[2])
        return v

    def gather_rows_side(j):
        v = est[SIDE + j]
        if j < 4:
            v = v + jnp.where(band == 1, roll(est[SIDE + j + 11], -SKEW[0]), 0.0)
            v = v + jnp.where(band == 2, roll(est[SIDE + j + 16], SKEW[2]), 0.0)
        if j >= 16:
            v = v + jnp.where(band == 1, roll(est[SIDE + j - 16], -SKEW[2]), 0.0)
        if 11 <= j < 15:
            v = v + jnp.where(band == 0, roll(est[SIDE + j - 11], SKEW[0]), 0.0)
        return jnp.where(mine_any, v, 0.0)

    near = [range(6, 15), range(0, 20), range(0, 9)]
    from_minus = (relx == 126) | (relx == 127) | (relx == 4) | (relx == 5)
    from_plus = (relx == 122) | (relx == 123) | (relx == 0) | (relx == 1)
    from_main_minus = (relx == 2) | (relx == 3)
    from_main_plus = (relx == 124) | (relx == 125)
    def first_tiles(j):
        side = gather_rows_side(j)
        s4, s_4 = roll(side, 4), roll(side, -4)
        add = jnp.where(from_minus, s4, jnp.where(from_plus, s_4, 0.0))
        exists = has_n if j < 2 else (has_s if j >= 18 else None)
        for g in range(3):
            if j not in near[g]:
                continue
            m = gather_rows(g, j)
            f = m + jnp.where(rel[g] < 2, s4, jnp.where(rel[g] >= 126, s_4, 0.0))
            cross = jnp.where(from_main_minus, roll(m, 4), jnp.where(from_main_plus, roll(m, -4), add))
            add = jnp.where(band == g, cross, add)
            if g == 1 and exists is not None:
                f = jnp.where(exists, f, 0.0)
            first[BASE[g] + j] = f
        f = side + add
        if exists is not None:
            f = jnp.where((band != 1) | exists, f, 0.0)
        first[SIDE + j] = f

    blocks(range(20), CHUNK[2], first_tiles)

    core_lane = ((relx >= 4) & (relx < 17)) | ((relx > 110) & (relx < 124))

    def emit_rhs(at, g, j, total, x):
        b = total - x
        if g == 3:
            keep = core_lane & mine_any
            use = []
            if 7 <= j <= 12:
                use.append((band == 0) & has_n)
            if 2 <= j <= 17:
                use.append(band == 1)
            if 2 <= j <= 7:
                use.append((band == 2) & has_s)
            if not use:
                b = zero
            else:
                any_use = use[0]
                for u in use[1:]:
                    any_use = any_use | u
                b = jnp.where(keep & any_use, b, 0.0)
        elif g == 0:
            b = jnp.where(has_n, b, 0.0) if 7 <= j <= 12 else zero
        elif g == 2:
            b = jnp.where(has_s, b, 0.0) if 2 <= j <= 7 else zero
        elif not 2 <= j <= 17:
            b = zero
        rhs[at] = b
        est[at] = tau0 * b

    blocks([0], 1, lambda _: stencil(first, rhs, near, emit_rhs))

    solve([range(7, 15), range(0, 20), range(0, 8)])

    def out_rows(j):
        side = est[SIDE + j]
        if j < 4:
            side = side + roll(est[SIDE + j + 11], -SKEW[0])
        if j >= 16:
            side = side + roll(est[SIDE + j - 16], -SKEW[2])
        v = first[BASE[1] + j] + gather_rows(1, j)
        v = v + jnp.where(lane < 2, roll(side, 4), jnp.where(lane >= 126, roll(side, -4), 0.0))
        out_ref[pl.ds(j - 2, NZ, stride=ROWS), :] = v

    blocks(range(2, 18), CHUNK[3], out_rows)

    for c in copies:
        c.wait_send()


def body(source, conduct, solid):
    flat = (NZ * ROWS, COLS)
    f32, i32 = jnp.float32, jnp.int32
    tile = (NZ, COLS)
    out = pl.pallas_call(
        kernel,
        out_shape=jax.ShapeDtypeStruct(flat, f32),
        in_specs=[pl.BlockSpec(memory_space=pltpu.HBM)] * 3,
        out_specs=pl.BlockSpec(memory_space=pltpu.VMEM),
        scratch_shapes=[
            pltpu.VMEM(flat, f32), pltpu.VMEM(flat, f32), pltpu.VMEM(flat, i32),
            pltpu.VMEM((2, 6, *tile), f32),
            pltpu.VMEM((2, *flat), f32), pltpu.VMEM((2, *flat), f32), pltpu.VMEM((2, *flat), i32),
            pltpu.VMEM((6, 6, *tile), f32),
            pltpu.VMEM((52, *tile), f32), pltpu.VMEM((21, *tile), f32),
            pltpu.VMEM((6, TILES, *tile), f32),
            pltpu.VMEM((TILES, *tile), f32), pltpu.VMEM((TILES, *tile), f32), pltpu.VMEM((TILES, *tile), f32),
            pltpu.SemaphoreType.DMA((3,)), pltpu.SemaphoreType.DMA((12,)), pltpu.SemaphoreType.DMA((12,)),
            pltpu.SemaphoreType.REGULAR((8,)),
        ],
        compiler_params=pltpu.CompilerParams(
            collective_id=0, has_side_effects=True, vmem_limit_bytes=16 * 1024 * 1024),
    )(*(pltpu.with_memory_space_constraint(x.reshape(flat), pltpu.HBM) for x in (source, conduct, solid)))
    return out.reshape(source.shape)


def solution(mesh):
    spec = P(None, "row", "aisle")
    return jax.shard_map(body, mesh=mesh, in_specs=(spec, spec, spec), out_specs=spec, check_vma=False)
```

```python
import functools
import math

import jax
import jax.numpy as jnp
from jax import lax
from jax.experimental import pallas as pl
from jax.experimental.pallas import tpu as pltpu
from jax.sharding import PartitionSpec as P

MESH = pl.DeviceIdType.MESH
NZ, ROWS, COLS = 8, 16, 128

MIDDLE, SPREAD, STEPS = 1.1, 0.9, 7
CHUNK = (4, 2, 4, 8, 2, 7)
ORDER = (4, 1, 7, 3, 5, 2, 6)
TAUS = tuple(1.0 / (MIDDLE + SPREAD * math.cos(math.pi * (2 * k - 1) / (2 * STEPS))) for k in ORDER)

FIRST_ROW = (-13, -2, 14)
LENGTH = (15, 20, 15)
SKEW = (40, 0, 88)
BASE = (0, 15, 35)
SIDE = 50
TILES = 70
K_ROWS = (range(-14, 2), range(-2, 18), range(14, 30))


def roll(x, by):
    by = by % COLS
    return x if by == 0 else pltpu.roll(x, by, 1)


def vroll(x, by):
    return pltpu.roll(x, by % NZ, 0)


def kernel(src_hbm, cond_hbm, solid_hbm, out_ref,
           own_src, own_cond, own_solid, to_side, ns_src, ns_cond, ns_solid, from_side,
           half, half_side, wgt, rhs, est, first,
           load_sem, send_sem, recv_sem, ready_sem):
    n_a, n_r = lax.axis_size("aisle"), lax.axis_size("row")
    a, r = lax.axis_index("aisle"), lax.axis_index("row")
    has_n, has_s = r > 0, r < n_r - 1

    def device(da, dr):
        return {"aisle": lax.rem(a + (da + n_a), n_a), "row": lax.rem(r + (dr + n_r), n_r)}

    loads = [
        pltpu.make_async_copy(h, v, load_sem.at[i])
        for i, (h, v) in enumerate(((cond_hbm, own_cond), (solid_hbm, own_solid), (src_hbm, own_src)))
    ]
    for c in loads:
        c.start()

    def order(pos_a, pos_r):
        plane = lax.rem(lax.div(pos_a, 2), 2) * 4 + lax.rem(pos_r, 4)
        return jnp.where((pos_a == 0) & (pos_r == 0), 15, plane * 4 + lax.rem(pos_a, 2) * 2)

    near_side = 1 - 2 * lax.rem(a, 2)
    sides = {"own": 0, "near": near_side, "far": -near_side}
    ways = [("own", 1), ("near", 0), ("near", 1), ("near", -1), ("own", -1), ("far", 0), ("far", 1), ("far", -1)]
    place = {w: i for i, w in enumerate(ways)}

    def order(pos_a, pos_r):
        plane = lax.rem(lax.div(pos_a, 2), 2) * 4 + lax.rem(pos_r, 4)
        return jnp.where((pos_a == 0) & (pos_r == 0), 15, plane * 4 + lax.rem(pos_a, 2) * 2)

    here_at = order(a, r)
    earlier, n_earlier = {}, 0
    for side, dr in ways:
        there = device(sides[side], dr)
        earlier[side, dr] = order(there["aisle"], there["row"]) < here_at
        n_earlier = n_earlier + earlier[side, dr].astype(jnp.int32)
    barrier = pltpu.get_barrier_semaphore()
    for w in ways:
        @pl.when(jnp.logical_not(earlier[w]))
        def _():
            pl.semaphore_signal(barrier, inc=1, device_id=device(sides[w[0]], w[1]), device_id_type=MESH)

    @pl.when(n_earlier > 0)
    def _():
        pl.semaphore_wait(barrier, n_earlier)

    for w in ways:
        @pl.when(earlier[w])
        def _():
            pl.semaphore_signal(ready_sem.at[place[w[0], -w[1]]], inc=1, device_id=device(sides[w[0]], w[1]), device_id_type=MESH)

    def blocks(indices, size, do):
        indices = list(indices)
        for at in range(0, len(indices), size):
            @pl.when(r >= 0)
            def _():
                for i in indices[at:at + size]:
                    do(i)

    lane = lax.broadcasted_iota(jnp.int32, (NZ, COLS), 1)
    level = lax.broadcasted_iota(jnp.int32, (NZ, COLS), 0)
    rel = [lax.rem(lane + (COLS - s), COLS) for s in SKEW]
    mine = [(q < 18) | (q >= 110) for q in rel]
    band = jnp.where(mine[0], 0, jnp.where(mine[2], 2, jnp.where(mine[1], 1, 3)))
    relx = jnp.where(mine[0], rel[0], jnp.where(mine[2], rel[2], jnp.where(mine[1], rel[1], 64)))
    code = band * COLS + relx
    zero = jnp.zeros((NZ, COLS), jnp.float32)
    one = jnp.ones((NZ, COLS), jnp.float32)

    def own_row(kind, row):
        rows = pl.ds(row, NZ, stride=ROWS)
        if kind == 0:
            return own_cond[rows, :]
        if kind == 1:
            return 0.05 + 20.0 * own_solid[rows, :].astype(jnp.float32)
        return own_src[rows, :]

    slot = lax.div(lane, 16)
    def pack(i):
        kind, half_of = divmod(i, 2)
        if half_of == 0:
            loads[kind].wait()
        west, east = zero, zero
        for s in range(8):
            v = own_row(kind, half_of * 8 + s)
            here = slot == s
            west = jnp.where(here, roll(v, 16 * s), west)
            east = jnp.where(here, roll(v, 16 * s + 14), east)
        to_side[0, i] = west
        to_side[1, i] = east

    blocks(range(6), CHUNK[4], pack)

    copies, n = {}, 0
    for side, dr in ways:
        if side == "own":
            w = 1 if dr < 0 else 0
            pairs = [(cond_hbm, ns_cond.at[w]), (solid_hbm, ns_solid.at[w]), (src_hbm, ns_src.at[w])]
        else:
            east = lax.div(sides[side] + 1, 2)
            pairs = [(to_side.at[east], from_side.at[3 * (1 - east) + 1 - dr])]
        copies[side, dr] = []
        for source, target in pairs:
            copies[side, dr].append(pltpu.make_async_remote_copy(
                src_ref=source, dst_ref=target, send_sem=send_sem.at[n], recv_sem=recv_sem.at[n],
                device_id=device(sides[side], dr), device_id_type=MESH))
            n += 1
    for w in ways[::-1]:
        @pl.when(earlier[w])
        def _():
            for c in copies[w]:
                c.start()
    def send_later(which):
        for w in which:
            @pl.when(jnp.logical_not(earlier[w]))
            def _():
                pl.semaphore_wait(ready_sem.at[place[w]], 1)
                for c in copies[w]:
                    c.start()

    send_later(ways)
    for dr in (1, -1):
        for c in copies["own", dr]:
            c.wait_recv()

    fill = (zero, one, zero)

    def main_row(kind, row):
        if 0 <= row < ROWS:
            return own_row(kind, row)
        w, exists = (0, has_n) if row < 0 else (1, has_s)
        rows = pl.ds(row % ROWS, NZ, stride=ROWS)
        if kind == 0:
            v = ns_cond[w, rows, :]
        elif kind == 1:
            v = 0.05 + 20.0 * ns_solid[w, rows, :].astype(jnp.float32)
        else:
            v = ns_src[w, rows, :]
        return jnp.where(exists, v, fill[kind])

    def side_start(kind, j, mains):
        tile = fill[kind]
        for g, m in mains.items():
            own = jnp.where(relx < 64, roll(m, 4), roll(m, -4))
            tile = jnp.where(edge == g, own, tile)
        return tile

    def strips(side, kind, j, tile):
        for g in range(3):
            row = FIRST_ROW[g] + j
            if row not in K_ROWS[g] or (kind and not 0 <= j < LENGTH[g]):
                continue
            if kind == 2 and not (row < 0, 0 <= row < ROWS, row >= ROWS)[g]:
                continue
            which, q = (0 if row < 0 else (1 if row < ROWS else 2)), row % ROWS
            v = from_side[first_of[side] + which, kind * 2 + q // 8]
            by = lax.rem(shift_of[side] + (SKEW[g] - 16 * (q % 8) + COLS), COLS)
            at = g if which == 1 else jnp.where((has_n, None, has_s)[which], g, 8)
            tile = jnp.where(strip_of[side] == at, pltpu.roll(v, by, 1), tile)
        return tile

    def finish(tile):
        return jnp.where(relx < 2, roll(tile, -4), jnp.where(relx >= 126, roll(tile, 4), tile))

    edge = jnp.where((relx == 2) | (relx == 3) | (relx == 124) | (relx == 125), band, 9)
    east_strip = (relx >= 4) & (relx < 18)
    west_strip = (relx >= 110) & (relx < 124)
    east_near = lax.div(near_side + 1, 2)
    east_of = {"near": east_near, "far": 1 - east_near}
    first_of = {k: 3 * e for k, e in east_of.items()}
    shift_of = {k: jnp.where(e == 1, 4, COLS - 18) for k, e in east_of.items()}
    strip_of = {k: jnp.where((east_strip & (e == 1)) | (west_strip & (e == 0)), band, 9) for k, e in east_of.items()}

    def hidx(g, j):
        return (0, 16, 36)[g] + j + (1 if g == 0 else 0)

    def conduct_tiles(j):
        mains = {}
        for g in range(3):
            row = FIRST_ROW[g] + j
            if row in K_ROWS[g]:
                mains[g] = roll(main_row(0, row), SKEW[g])
                half[hidx(g, j)] = 0.5 * mains[g]
        half_side[j + 1] = side_start(0, j, mains)

    blocks(range(-1, 20), CHUNK[0], conduct_tiles)


    top, bottom = level == NZ - 1, level == 0

    def vertical(h):
        return h + jnp.where(top, 0.0, vroll(h, -1)), h + jnp.where(bottom, 0.0, vroll(h, 1))

    def main_tiles(j):
        shifts = {}
        for g in range(3):
            if j >= LENGTH[g]:
                continue
            row, at = FIRST_ROW[g] + j, BASE[g] + j
            shifts[g] = s = roll(main_row(1, row), SKEW[g])
            h = half[hidx(g, j)]
            vp, vm = vertical(h)
            rp = h + (half[hidx(g, j + 1)] if row + 1 in K_ROWS[g] else zero)
            rm = h + (half[hidx(g, j - 1)] if row - 1 in K_ROWS[g] else zero)
            est[at] = (((s + vp) + vm) + rp) + rm
            wgt[0, at] = jnp.where(top, 0.0, vp)
            wgt[1, at] = jnp.where(bottom, 0.0, vm)
            wgt[2, at] = rp
            wgt[3, at] = rm
            if (row < 0, 0 <= row < ROWS, row >= ROWS)[g]:
                rhs[at] = roll(main_row(2, row), SKEW[g])
            else:
                rhs[at] = zero
        est[SIDE + j] = side_start(1, j, shifts)
        rhs[SIDE + j] = zero

    blocks(range(20), CHUNK[1], main_tiles)


    def side_strips(side):
        def do(j):
            half_side[j + 1] = strips(side, 0, j, half_side[j + 1])
            if j >= 0:
                est[SIDE + j] = strips(side, 1, j, est[SIDE + j])
                rhs[SIDE + j] = strips(side, 2, j, rhs[SIDE + j])
        return do

    for side, dr in ways:
        if side == "near":
            for c in copies[side, dr]:
                c.wait_recv()
    blocks(range(-1, 20), CHUNK[5], side_strips("near"))
    for side, dr in ways:
        if side == "far":
            for c in copies[side, dr]:
                c.wait_recv()
    copies = [c for w in ways for c in copies[w]]

    blocks(range(-1, 20), CHUNK[5], side_strips("far"))

    def finish_tiles(j):
        half_side[j + 1] = 0.5 * finish(half_side[j + 1])
        if j >= 0:
            est[SIDE + j] = finish(est[SIDE + j])

    blocks(range(-1, 20), CHUNK[5], finish_tiles)

    def around_cols(mains, side):
        sp, sm = roll(side, -1), roll(side, 1)
        out, plus, minus = {}, sp, sm
        for g, m in mains.items():
            mp, mm = roll(m, -1), roll(m, 1)
            out[g] = (jnp.where(rel[g] == 127, sp, mp), jnp.where(rel[g] == 0, sm, mm))
            plus = jnp.where(code == g * COLS + 127, mp, plus)
            minus = jnp.where(code == g * COLS, mm, minus)
        out[3] = (plus, minus)
        return out

    no_plus = (relx == 1) | (relx == 125)
    no_minus = (relx == 2) | (relx == 126)
    live = (band < 3) & ((relx < 17) | (relx > 110))

    tau0 = TAUS[0]

    def weight_tiles(j):
        bands = [g for g in range(3) if j < LENGTH[g]]
        mains = {g: half[hidx(g, j)] for g in bands}
        h = half_side[j + 1]
        cols = around_cols(mains, h)
        for g in bands:
            at = BASE[g] + j
            cp, cm = mains[g] + cols[g][0], mains[g] + cols[g][1]
            inverse = 1.0 / ((est[at] + cp) + cm)
            for i in range(4):
                wgt[i, at] = inverse * wgt[i, at]
            wgt[4, at] = inverse * cp
            wgt[5, at] = inverse * cm
            b = inverse * rhs[at]
            rhs[at] = b
            est[at] = tau0 * b
        at = SIDE + j
        up = half_side[j]
        if j == 0:
            up = jnp.where(band == 0, up, 0.0)
        vp, vm = vertical(h)
        rp = h + (half_side[j + 2] if j < 19 else zero)
        rm = h + up
        cp = h + jnp.where(no_plus, 0.0, cols[3][0])
        cm = h + jnp.where(no_minus, 0.0, cols[3][1])
        inverse = 1.0 / ((((((est[at] + vp) + vm) + rp) + rm) + cp) + cm)
        inverse = jnp.where(live if len(bands) == 3 else live & (band == 1), inverse, 0.0)
        wgt[0, at] = jnp.where(top, 0.0, inverse * vp)
        wgt[1, at] = jnp.where(bottom, 0.0, inverse * vm)
        wgt[2, at] = inverse * rp
        wgt[3, at] = inverse * rm
        wgt[4, at] = jnp.where(no_plus, 0.0, inverse * cp)
        wgt[5, at] = jnp.where(no_minus, 0.0, inverse * cm)
        b = inverse * rhs[at]
        rhs[at] = b
        est[at] = tau0 * b

    blocks(range(20), CHUNK[1], weight_tiles)

    def stencil(ref, b, spans, emit):
        def load(g, j):
            if g == 3:
                return ref[SIDE + j] if 0 <= j < 20 else None
            return ref[BASE[g] + j] if j in spans[g] else None

        old = {(g, j): load(g, j) for g in range(4) for j in (-1, 0)}
        for j in range(20):
            for g in range(4):
                old[g, j + 1] = load(g, j + 1)
            mains = {g: old[g, j] for g in range(3) if old[g, j] is not None}
            cols = around_cols(mains, old[3, j])
            for g in (*mains, 3):
                at = (SIDE if g == 3 else BASE[g]) + j
                x = old[g, j]
                plus, minus = cols[g]
                total = b[at] + wgt[0, at] * vroll(x, -1)
                other = wgt[1, at] * vroll(x, 1)
                if old[g, j + 1] is not None:
                    total = total + wgt[2, at] * old[g, j + 1]
                if old[g, j - 1] is not None:
                    other = other + wgt[3, at] * old[g, j - 1]
                total = total + wgt[4, at] * plus
                other = other + wgt[5, at] * minus
                emit(at, g, j, total + other, x)

    def solve(spans):
        def sweep(t, carry):
            tau = jnp.float32(TAUS[STEPS - 1])
            for i in range(STEPS - 2, 0, -1):
                tau = jnp.where(t == i, jnp.float32(TAUS[i]), tau)

            def emit(at, g, j, total, x):
                est[at] = x + tau * (total - x)

            stencil(est, rhs, spans, emit)
            return carry

        lax.fori_loop(1, STEPS, sweep, 0)

    full = [range(n) for n in LENGTH]
    solve(full)

    def gather_rows(g, j):
        v = est[BASE[g] + j]
        if g == 1 and j < 4:
            v = v + roll(est[BASE[0] + j + 11], -SKEW[0])
        if g == 1 and j >= 16:
            v = v + roll(est[BASE[2] + j - 16], -SKEW[2])
        if g == 0 and j >= 11:
            v = v + roll(est[BASE[1] + j - 11], SKEW[0])
        if g == 2 and j < 4:
            v = v + roll(est[BASE[1] + j + 16], SKEW[2])
        return v

    def gather_rows_side(j):
        v = est[SIDE + j]
        if j < 4:
            v = v + jnp.where(band == 1, roll(est[SIDE + j + 11], -SKEW[0]), 0.0)
            v = v + jnp.where(band == 2, roll(est[SIDE + j + 16], SKEW[2]), 0.0)
        if j >= 16:
            v = v + jnp.where(band == 1, roll(est[SIDE + j - 16], -SKEW[2]), 0.0)
        if 11 <= j < 15:
            v = v + jnp.where(band == 0, roll(est[SIDE + j - 11], SKEW[0]), 0.0)
        return v

    near = [range(6, 15), range(0, 20), range(0, 9)]
    def among(*values):
        return functools.reduce(jnp.logical_or, [relx == v for v in values])

    origin = jnp.where(among(126, 127, 4, 5), 1, jnp.where(among(122, 123, 0, 1), 2, jnp.where(among(2, 3), 3, jnp.where(among(124, 125), 4, 0))))
    crossing = jnp.where(origin >= 3, band, 9)

    def first_tiles(j):
        side = gather_rows_side(j)
        s4, s_4 = roll(side, 4), roll(side, -4)
        add = jnp.where(origin == 1, s4, jnp.where(origin == 2, s_4, 0.0))
        exists = has_n if j < 2 else (has_s if j >= 18 else None)
        for g in range(3):
            if j not in near[g]:
                continue
            m = gather_rows(g, j)
            f = m + jnp.where(rel[g] < 2, s4, jnp.where(rel[g] >= 126, s_4, 0.0))
            add = jnp.where(crossing == g, jnp.where(origin == 3, roll(m, 4), roll(m, -4)), add)
            if g == 1 and exists is not None:
                f = jnp.where(exists, f, 0.0)
            first[BASE[g] + j] = f
        f = side + add
        if exists is not None:
            f = jnp.where((band != 1) | exists, f, 0.0)
        first[SIDE + j] = f

    blocks(range(20), CHUNK[2], first_tiles)

    core = jnp.where(((relx >= 4) & (relx < 17)) | ((relx > 110) & (relx < 124)), band, 9)
    to_north, to_south = jnp.where(has_n, 0, 8), jnp.where(has_s, 2, 8)

    def emit_rhs(at, g, j, total, x):
        b = total - x
        if g == 3:
            use = []
            if 7 <= j <= 12:
                use.append(core == to_north)
            if 2 <= j <= 17:
                use.append(core == 1)
            if 2 <= j <= 7:
                use.append(core == to_south)
            b = jnp.where(functools.reduce(jnp.logical_or, use), b, 0.0) if use else zero
        elif g == 0:
            b = jnp.where(has_n, b, 0.0) if 7 <= j <= 12 else zero
        elif g == 2:
            b = jnp.where(has_s, b, 0.0) if 2 <= j <= 7 else zero
        elif not 2 <= j <= 17:
            b = zero
        rhs[at] = b
        est[at] = tau0 * b

    blocks([0], 1, lambda _: stencil(first, rhs, near, emit_rhs))

    solve([range(7, 15), range(0, 20), range(0, 8)])

    def out_rows(j):
        side = est[SIDE + j]
        if j < 4:
            side = side + roll(est[SIDE + j + 11], -SKEW[0])
        if j >= 16:
            side = side + roll(est[SIDE + j - 16], -SKEW[2])
        v = first[BASE[1] + j] + gather_rows(1, j)
        v = v + jnp.where(lane < 2, roll(side, 4), jnp.where(lane >= 126, roll(side, -4), 0.0))
        out_ref[pl.ds(j - 2, NZ, stride=ROWS), :] = v

    blocks(range(2, 18), CHUNK[3], out_rows)

    for c in copies:
        c.wait_send()


def body(source, conduct, solid):
    flat = (NZ * ROWS, COLS)
    f32, i32 = jnp.float32, jnp.int32
    tile = (NZ, COLS)
    out = pl.pallas_call(
        kernel,
        out_shape=jax.ShapeDtypeStruct(flat, f32),
        in_specs=[pl.BlockSpec(memory_space=pltpu.HBM)] * 3,
        out_specs=pl.BlockSpec(memory_space=pltpu.VMEM),
        scratch_shapes=[
            pltpu.VMEM(flat, f32), pltpu.VMEM(flat, f32), pltpu.VMEM(flat, i32),
            pltpu.VMEM((2, 6, *tile), f32),
            pltpu.VMEM((2, *flat), f32), pltpu.VMEM((2, *flat), f32), pltpu.VMEM((2, *flat), i32),
            pltpu.VMEM((6, 6, *tile), f32),
            pltpu.VMEM((52, *tile), f32), pltpu.VMEM((21, *tile), f32),
            pltpu.VMEM((6, TILES, *tile), f32),
            pltpu.VMEM((TILES, *tile), f32), pltpu.VMEM((TILES, *tile), f32), pltpu.VMEM((TILES, *tile), f32),
            pltpu.SemaphoreType.DMA((3,)), pltpu.SemaphoreType.DMA((12,)), pltpu.SemaphoreType.DMA((12,)),
            pltpu.SemaphoreType.REGULAR((8,)),
        ],
        compiler_params=pltpu.CompilerParams(
            collective_id=0, has_side_effects=True, vmem_limit_bytes=16 * 1024 * 1024),
    )(*(pltpu.with_memory_space_constraint(x.reshape(flat), pltpu.HBM) for x in (source, conduct, solid)))
    return out.reshape(source.shape)


def solution(mesh):
    spec = P(None, "row", "aisle")
    return jax.shard_map(body, mesh=mesh, in_specs=(spec, spec, spec), out_specs=spec, check_vma=False)
```

```python
import functools
import math

import jax
import jax.numpy as jnp
from jax import lax
from jax.experimental import pallas as pl
from jax.experimental.pallas import tpu as pltpu
from jax.sharding import PartitionSpec as P

MESH = pl.DeviceIdType.MESH
NZ, ROWS, COLS = 8, 16, 128

MIDDLE, SPREAD, STEPS = 1.1, 0.9, 7
CHUNK = (4, 2, 4, 8, 2, 7)
ORDER = (4, 1, 7, 3, 5, 2, 6)
TAUS = tuple(1.0 / (MIDDLE + SPREAD * math.cos(math.pi * (2 * k - 1) / (2 * STEPS))) for k in ORDER)

FIRST_ROW = (-13, -2, 14)
LENGTH = (15, 20, 15)
SKEW = (40, 0, 88)
BASE = (0, 15, 35)
SIDE = 50
TILES = 70
K_ROWS = (range(-14, 2), range(-2, 18), range(14, 30))


def roll(x, by):
    by = by % COLS
    return x if by == 0 else pltpu.roll(x, by, 1)


def vroll(x, by):
    return pltpu.roll(x, by % NZ, 0)


def kernel(src_hbm, cond_hbm, solid_hbm, out_ref,
           own_src, own_cond, own_solid, to_side, ns_src, ns_cond, ns_solid, from_side,
           half, half_side, wgt, rhs, est, first,
           load_sem, send_sem, recv_sem, ready_sem):
    n_a, n_r = lax.axis_size("aisle"), lax.axis_size("row")
    a, r = lax.axis_index("aisle"), lax.axis_index("row")
    has_n, has_s = r > 0, r < n_r - 1

    def device(da, dr):
        return {"aisle": lax.rem(a + (da + n_a), n_a), "row": lax.rem(r + (dr + n_r), n_r)}

    loads = [
        pltpu.make_async_copy(h, v, load_sem.at[i])
        for i, (h, v) in enumerate(((cond_hbm, own_cond), (solid_hbm, own_solid), (src_hbm, own_src)))
    ]
    for c in loads:
        c.start()

    def order(pos_a, pos_r):
        plane = lax.rem(lax.div(pos_a, 2), 2) * 4 + lax.rem(pos_r, 4)
        return jnp.where((pos_a == 0) & (pos_r == 0), 15, plane * 4 + lax.rem(pos_a, 2) * 2)

    near_side = 1 - 2 * lax.rem(a, 2)
    sides = {"own": 0, "near": near_side, "far": -near_side}
    ways = [("own", 1), ("near", 0), ("near", 1), ("near", -1), ("own", -1), ("far", 0), ("far", 1), ("far", -1)]
    place = {w: i for i, w in enumerate(ways)}

    def order(pos_a, pos_r):
        plane = lax.rem(lax.div(pos_a, 2), 2) * 4 + lax.rem(pos_r, 4)
        return jnp.where((pos_a == 0) & (pos_r == 0), 15, plane * 4 + lax.rem(pos_a, 2) * 2)

    here_at = order(a, r)
    earlier, n_earlier = {}, 0
    for side, dr in ways:
        there = device(sides[side], dr)
        earlier[side, dr] = order(there["aisle"], there["row"]) < here_at
        n_earlier = n_earlier + earlier[side, dr].astype(jnp.int32)
    barrier = pltpu.get_barrier_semaphore()
    for w in ways:
        @pl.when(jnp.logical_not(earlier[w]))
        def _():
            pl.semaphore_signal(barrier, inc=1, device_id=device(sides[w[0]], w[1]), device_id_type=MESH)

    @pl.when(n_earlier > 0)
    def _():
        pl.semaphore_wait(barrier, n_earlier)

    for w in ways:
        @pl.when(earlier[w])
        def _():
            pl.semaphore_signal(ready_sem.at[place[w[0], -w[1]]], inc=1, device_id=device(sides[w[0]], w[1]), device_id_type=MESH)

    def blocks(indices, size, do):
        indices = list(indices)
        for at in range(0, len(indices), size):
            @pl.when(r >= 0)
            def _():
                for i in indices[at:at + size]:
                    do(i)

    lane = lax.broadcasted_iota(jnp.int32, (NZ, COLS), 1)
    level = lax.broadcasted_iota(jnp.int32, (NZ, COLS), 0)
    rel = [lax.rem(lane + (COLS - s), COLS) for s in SKEW]
    mine = [(q < 18) | (q >= 110) for q in rel]
    band = jnp.where(mine[0], 0, jnp.where(mine[2], 2, jnp.where(mine[1], 1, 3)))
    relx = jnp.where(mine[0], rel[0], jnp.where(mine[2], rel[2], jnp.where(mine[1], rel[1], 64)))
    code = band * COLS + relx
    zero = jnp.zeros((NZ, COLS), jnp.float32)
    one = jnp.ones((NZ, COLS), jnp.float32)

    def own_row(kind, row):
        rows = pl.ds(row, NZ, stride=ROWS)
        if kind == 0:
            return own_cond[rows, :]
        if kind == 1:
            return 0.05 + 20.0 * own_solid[rows, :].astype(jnp.float32)
        return own_src[rows, :]

    slot = lax.div(lane, 16)
    def pack(i):
        kind, half_of = divmod(i, 2)
        if half_of == 0:
            loads[kind].wait()
        west, east = zero, zero
        for s in range(8):
            v = own_row(kind, half_of * 8 + s)
            here = slot == s
            west = jnp.where(here, roll(v, 16 * s), west)
            east = jnp.where(here, roll(v, 16 * s + 14), east)
        to_side[0, i] = west
        to_side[1, i] = east

    blocks(range(6), CHUNK[4], pack)

    copies, n = {}, 0
    for side, dr in ways:
        if side == "own":
            w = 1 if dr < 0 else 0
            pairs = [(cond_hbm, ns_cond.at[w]), (solid_hbm, ns_solid.at[w]), (src_hbm, ns_src.at[w])]
        else:
            east = lax.div(sides[side] + 1, 2)
            pairs = [(to_side.at[east], from_side.at[3 * (1 - east) + 1 - dr])]
        copies[side, dr] = []
        for source, target in pairs:
            copies[side, dr].append(pltpu.make_async_remote_copy(
                src_ref=source, dst_ref=target, send_sem=send_sem.at[n], recv_sem=recv_sem.at[n],
                device_id=device(sides[side], dr), device_id_type=MESH))
            n += 1
    for w in ways[::-1]:
        @pl.when(earlier[w])
        def _():
            for c in copies[w]:
                c.start()
    def send_later(which):
        for w in which:
            @pl.when(jnp.logical_not(earlier[w]))
            def _():
                pl.semaphore_wait(ready_sem.at[place[w]], 1)
                for c in copies[w]:
                    c.start()

    send_later(ways)
    for dr in (1, -1):
        for c in copies["own", dr]:
            c.wait_recv()

    fill = (zero, one, zero)

    def main_row(kind, row):
        if 0 <= row < ROWS:
            return own_row(kind, row)
        w, exists = (0, has_n) if row < 0 else (1, has_s)
        rows = pl.ds(row % ROWS, NZ, stride=ROWS)
        if kind == 0:
            v = ns_cond[w, rows, :]
        elif kind == 1:
            v = 0.05 + 20.0 * ns_solid[w, rows, :].astype(jnp.float32)
        else:
            v = ns_src[w, rows, :]
        return jnp.where(exists, v, fill[kind])

    def side_start(kind, j, mains):
        tile = fill[kind]
        for g, m in mains.items():
            own = jnp.where(relx < 64, roll(m, 4), roll(m, -4))
            tile = jnp.where(edge == g, own, tile)
        return tile

    def strips(side, kind, j, tile):
        for g in range(3):
            row = FIRST_ROW[g] + j
            if row not in K_ROWS[g] or (kind and not 0 <= j < LENGTH[g]):
                continue
            if kind == 2 and not (row < 0, 0 <= row < ROWS, row >= ROWS)[g]:
                continue
            which, q = (0 if row < 0 else (1 if row < ROWS else 2)), row % ROWS
            v = from_side[first_of[side] + which, kind * 2 + q // 8]
            by = lax.rem(shift_of[side] + (SKEW[g] - 16 * (q % 8) + COLS), COLS)
            at = g if which == 1 else jnp.where((has_n, None, has_s)[which], g, 8)
            tile = jnp.where(strip_of[side] == at, pltpu.roll(v, by, 1), tile)
        return tile

    def finish(tile):
        return jnp.where(relx < 2, roll(tile, -4), jnp.where(relx >= 126, roll(tile, 4), tile))

    edge = jnp.where((relx == 2) | (relx == 3) | (relx == 124) | (relx == 125), band, 9)
    east_strip = (relx >= 4) & (relx < 18)
    west_strip = (relx >= 110) & (relx < 124)
    east_near = lax.div(near_side + 1, 2)
    east_of = {"near": east_near, "far": 1 - east_near}
    first_of = {k: 3 * e for k, e in east_of.items()}
    shift_of = {k: jnp.where(e == 1, 4, COLS - 18) for k, e in east_of.items()}
    strip_of = {k: jnp.where((east_strip & (e == 1)) | (west_strip & (e == 0)), band, 9) for k, e in east_of.items()}

    def hidx(g, j):
        return (0, 16, 36)[g] + j + (1 if g == 0 else 0)

    def conduct_tiles(j):
        mains = {}
        for g in range(3):
            row = FIRST_ROW[g] + j
            if row in K_ROWS[g]:
                mains[g] = roll(main_row(0, row), SKEW[g])
                half[hidx(g, j)] = 0.5 * mains[g]
        half_side[j + 1] = side_start(0, j, mains)

    blocks(range(-1, 20), CHUNK[0], conduct_tiles)


    top, bottom = level == NZ - 1, level == 0

    def vertical(h):
        return h + jnp.where(top, 0.0, vroll(h, -1)), h + jnp.where(bottom, 0.0, vroll(h, 1))

    def main_tiles(j):
        shifts = {}
        for g in range(3):
            if j >= LENGTH[g]:
                continue
            row, at = FIRST_ROW[g] + j, BASE[g] + j
            shifts[g] = s = roll(main_row(1, row), SKEW[g])
            h = half[hidx(g, j)]
            vp, vm = vertical(h)
            rp = h + (half[hidx(g, j + 1)] if row + 1 in K_ROWS[g] else zero)
            rm = h + (half[hidx(g, j - 1)] if row - 1 in K_ROWS[g] else zero)
            est[at] = (((s + vp) + vm) + rp) + rm
            wgt[0, at] = jnp.where(top, 0.0, vp)
            wgt[1, at] = jnp.where(bottom, 0.0, vm)
            wgt[2, at] = rp
            wgt[3, at] = rm
            if (row < 0, 0 <= row < ROWS, row >= ROWS)[g]:
                rhs[at] = roll(main_row(2, row), SKEW[g])
            else:
                rhs[at] = zero
        est[SIDE + j] = side_start(1, j, shifts)
        rhs[SIDE + j] = zero

    blocks(range(20), CHUNK[1], main_tiles)


    def side_strips(side):
        def do(j):
            half_side[j + 1] = strips(side, 0, j, half_side[j + 1])
            if j >= 0:
                est[SIDE + j] = strips(side, 1, j, est[SIDE + j])
                rhs[SIDE + j] = strips(side, 2, j, rhs[SIDE + j])
        return do

    for side, dr in ways:
        if side == "near":
            for c in copies[side, dr]:
                c.wait_recv()
    blocks(range(-1, 20), CHUNK[5], side_strips("near"))
    for side, dr in ways:
        if side == "far":
            for c in copies[side, dr]:
                c.wait_recv()
    copies = [c for w in ways for c in copies[w]]

    blocks(range(-1, 20), CHUNK[5], side_strips("far"))

    def finish_tiles(j):
        half_side[j + 1] = 0.5 * finish(half_side[j + 1])
        if j >= 0:
            est[SIDE + j] = finish(est[SIDE + j])

    blocks(range(-1, 20), CHUNK[5], finish_tiles)

    def around_cols(mains, side):
        sp, sm = roll(side, -1), roll(side, 1)
        out, plus, minus = {}, sp, sm
        for g, m in mains.items():
            mp, mm = roll(m, -1), roll(m, 1)
            out[g] = (jnp.where(rel[g] == 127, sp, mp), jnp.where(rel[g] == 0, sm, mm))
            plus = jnp.where(code == g * COLS + 127, mp, plus)
            minus = jnp.where(code == g * COLS, mm, minus)
        out[3] = (plus, minus)
        return out

    no_plus = (relx == 1) | (relx == 125)
    no_minus = (relx == 2) | (relx == 126)
    live = (band < 3) & ((relx < 17) | (relx > 110))

    tau0 = TAUS[0]

    def weight_tiles(j):
        bands = [g for g in range(3) if j < LENGTH[g]]
        mains = {g: half[hidx(g, j)] for g in bands}
        h = half_side[j + 1]
        cols = around_cols(mains, h)
        for g in bands:
            at = BASE[g] + j
            cp, cm = mains[g] + cols[g][0], mains[g] + cols[g][1]
            inverse = 1.0 / ((est[at] + cp) + cm)
            for i in range(4):
                wgt[i, at] = inverse * wgt[i, at]
            wgt[4, at] = inverse * cp
            wgt[5, at] = inverse * cm
            b = inverse * rhs[at]
            rhs[at] = b
            est[at] = tau0 * b
        at = SIDE + j
        up = half_side[j]
        if j == 0:
            up = jnp.where(band == 0, up, 0.0)
        vp, vm = vertical(h)
        rp = h + (half_side[j + 2] if j < 19 else zero)
        rm = h + up
        cp = h + jnp.where(no_plus, 0.0, cols[3][0])
        cm = h + jnp.where(no_minus, 0.0, cols[3][1])
        inverse = 1.0 / ((((((est[at] + vp) + vm) + rp) + rm) + cp) + cm)
        inverse = jnp.where(live if len(bands) == 3 else live & (band == 1), inverse, 0.0)
        wgt[0, at] = jnp.where(top, 0.0, inverse * vp)
        wgt[1, at] = jnp.where(bottom, 0.0, inverse * vm)
        wgt[2, at] = inverse * rp
        wgt[3, at] = inverse * rm
        wgt[4, at] = jnp.where(no_plus, 0.0, inverse * cp)
        wgt[5, at] = jnp.where(no_minus, 0.0, inverse * cm)
        b = inverse * rhs[at]
        rhs[at] = b
        est[at] = tau0 * b

    blocks(range(20), CHUNK[1], weight_tiles)

    def stencil(ref, b, spans, emit):
        def load(g, j):
            if g == 3:
                return ref[SIDE + j] if 0 <= j < 20 else None
            return ref[BASE[g] + j] if j in spans[g] else None

        old = {(g, j): load(g, j) for g in range(4) for j in (-1, 0)}
        for j in range(20):
            for g in range(4):
                old[g, j + 1] = load(g, j + 1)
            mains = {g: old[g, j] for g in range(3) if old[g, j] is not None}
            cols = around_cols(mains, old[3, j])
            for g in (*mains, 3):
                at = (SIDE if g == 3 else BASE[g]) + j
                x = old[g, j]
                plus, minus = cols[g]
                total = b[at] + wgt[0, at] * vroll(x, -1)
                other = wgt[1, at] * vroll(x, 1)
                if old[g, j + 1] is not None:
                    total = total + wgt[2, at] * old[g, j + 1]
                if old[g, j - 1] is not None:
                    other = other + wgt[3, at] * old[g, j - 1]
                total = total + wgt[4, at] * plus
                other = other + wgt[5, at] * minus
                emit(at, g, j, total + other, x)

    def solve(spans, begin, end):
        def sweep(t, carry):
            tau = jnp.float32(TAUS[STEPS - 1])
            for i in range(STEPS - 2, 0, -1):
                tau = jnp.where(t == i, jnp.float32(TAUS[i]), tau)

            def emit(at, g, j, total, x):
                est[at] = x + tau * (total - x)

            stencil(est, rhs, spans, emit)
            return carry

        lax.fori_loop(begin, end, sweep, 0)

    full = [range(n) for n in LENGTH]
    solve(full, 1, 4)
    solve([range(3, 15), range(0, 20), range(0, 12)], 4, STEPS)

    def gather_rows(g, j):
        v = est[BASE[g] + j]
        if g == 1 and j < 4:
            v = v + roll(est[BASE[0] + j + 11], -SKEW[0])
        if g == 1 and j >= 16:
            v = v + roll(est[BASE[2] + j - 16], -SKEW[2])
        if g == 0 and j >= 11:
            v = v + roll(est[BASE[1] + j - 11], SKEW[0])
        if g == 2 and j < 4:
            v = v + roll(est[BASE[1] + j + 16], SKEW[2])
        return v

    def gather_rows_side(j):
        v = est[SIDE + j]
        if j < 4:
            v = v + jnp.where(band == 1, roll(est[SIDE + j + 11], -SKEW[0]), 0.0)
            v = v + jnp.where(band == 2, roll(est[SIDE + j + 16], SKEW[2]), 0.0)
        if j >= 16:
            v = v + jnp.where(band == 1, roll(est[SIDE + j - 16], -SKEW[2]), 0.0)
        if 11 <= j < 15:
            v = v + jnp.where(band == 0, roll(est[SIDE + j - 11], SKEW[0]), 0.0)
        return v

    near = [range(6, 15), range(0, 20), range(0, 9)]
    def among(*values):
        return functools.reduce(jnp.logical_or, [relx == v for v in values])

    origin = jnp.where(among(126, 127, 4, 5), 1, jnp.where(among(122, 123, 0, 1), 2, jnp.where(among(2, 3), 3, jnp.where(among(124, 125), 4, 0))))
    crossing = jnp.where(origin >= 3, band, 9)

    def first_tiles(j):
        side = gather_rows_side(j)
        s4, s_4 = roll(side, 4), roll(side, -4)
        add = jnp.where(origin == 1, s4, jnp.where(origin == 2, s_4, 0.0))
        exists = has_n if j < 2 else (has_s if j >= 18 else None)
        for g in range(3):
            if j not in near[g]:
                continue
            m = gather_rows(g, j)
            f = m + jnp.where(rel[g] < 2, s4, jnp.where(rel[g] >= 126, s_4, 0.0))
            add = jnp.where(crossing == g, jnp.where(origin == 3, roll(m, 4), roll(m, -4)), add)
            if g == 1 and exists is not None:
                f = jnp.where(exists, f, 0.0)
            first[BASE[g] + j] = f
        f = side + add
        if exists is not None:
            f = jnp.where((band != 1) | exists, f, 0.0)
        first[SIDE + j] = f

    blocks(range(20), CHUNK[2], first_tiles)

    core = jnp.where(((relx >= 4) & (relx < 17)) | ((relx > 110) & (relx < 124)), band, 9)
    to_north, to_south = jnp.where(has_n, 0, 8), jnp.where(has_s, 2, 8)

    def emit_rhs(at, g, j, total, x):
        b = total - x
        if g == 3:
            use = []
            if 7 <= j <= 12:
                use.append(core == to_north)
            if 2 <= j <= 17:
                use.append(core == 1)
            if 2 <= j <= 7:
                use.append(core == to_south)
            b = jnp.where(functools.reduce(jnp.logical_or, use), b, 0.0) if use else zero
        elif g == 0:
            b = jnp.where(has_n, b, 0.0) if 7 <= j <= 12 else zero
        elif g == 2:
            b = jnp.where(has_s, b, 0.0) if 2 <= j <= 7 else zero
        elif not 2 <= j <= 17:
            b = zero
        rhs[at] = b
        est[at] = tau0 * b

    blocks([0], 1, lambda _: stencil(first, rhs, near, emit_rhs))

    solve([range(7, 15), range(0, 20), range(0, 8)], 1, 4)
    solve([range(10, 15), range(0, 20), range(0, 5)], 4, STEPS)

    def out_rows(j):
        side = est[SIDE + j]
        if j < 4:
            side = side + roll(est[SIDE + j + 11], -SKEW[0])
        if j >= 16:
            side = side + roll(est[SIDE + j - 16], -SKEW[2])
        v = first[BASE[1] + j] + gather_rows(1, j)
        v = v + jnp.where(lane < 2, roll(side, 4), jnp.where(lane >= 126, roll(side, -4), 0.0))
        out_ref[pl.ds(j - 2, NZ, stride=ROWS), :] = v

    blocks(range(2, 18), CHUNK[3], out_rows)

    for c in copies:
        c.wait_send()


def body(source, conduct, solid):
    flat = (NZ * ROWS, COLS)
    f32, i32 = jnp.float32, jnp.int32
    tile = (NZ, COLS)
    out = pl.pallas_call(
        kernel,
        out_shape=jax.ShapeDtypeStruct(flat, f32),
        in_specs=[pl.BlockSpec(memory_space=pltpu.HBM)] * 3,
        out_specs=pl.BlockSpec(memory_space=pltpu.VMEM),
        scratch_shapes=[
            pltpu.VMEM(flat, f32), pltpu.VMEM(flat, f32), pltpu.VMEM(flat, i32),
            pltpu.VMEM((2, 6, *tile), f32),
            pltpu.VMEM((2, *flat), f32), pltpu.VMEM((2, *flat), f32), pltpu.VMEM((2, *flat), i32),
            pltpu.VMEM((6, 6, *tile), f32),
            pltpu.VMEM((52, *tile), f32), pltpu.VMEM((21, *tile), f32),
            pltpu.VMEM((6, TILES, *tile), f32),
            pltpu.VMEM((TILES, *tile), f32), pltpu.VMEM((TILES, *tile), f32), pltpu.VMEM((TILES, *tile), f32),
            pltpu.SemaphoreType.DMA((3,)), pltpu.SemaphoreType.DMA((12,)), pltpu.SemaphoreType.DMA((12,)),
            pltpu.SemaphoreType.REGULAR((8,)),
        ],
        compiler_params=pltpu.CompilerParams(
            collective_id=0, has_side_effects=True, vmem_limit_bytes=16 * 1024 * 1024),
    )(*(pltpu.with_memory_space_constraint(x.reshape(flat), pltpu.HBM) for x in (source, conduct, solid)))
    return out.reshape(source.shape)


def solution(mesh):
    spec = P(None, "row", "aisle")
    return jax.shard_map(body, mesh=mesh, in_specs=(spec, spec, spec), out_specs=spec, check_vma=False)
```
